128 devices in a mesh: gx: 8 (over x_hi, z), gy: 16 (over y, x_lo, core).
Axes of the slice: x: 4 (x_hi: 2, x_lo: 2; x = x_hi * 2 + x_lo), y: 4, z: 4, core: 2. Of those that a mesh axis runs over, the one named last changes fastest.
Arguments:
- fine_state: float32 [9, 16, 512, 2048], P(None, None, 'gx', 'gy'), may hold values from -6 to 6
- fine_medium: float32 [3, 16, 512, 2048], P(None, None, 'gx', 'gy'), may hold values from 0.5 to 2
- coarse_state: float32 [9, 8, 256, 1024], P(None, None, 'gy', 'gx'), may hold values from -6 to 6
- coarse_medium: float32 [3, 8, 256, 1024], P(None, None, 'gy', 'gx'), may hold values from 0.5 to 2
- coarse_past: float32 [9, 2, 256, 1024], P(None, None, 'gy', 'gx'), may hold values from -6 to 6
- parent_rows: int32 [512], P('gx'), may hold values from 0 to 255, as said below
- parent_cols: int32 [2048], P('gy'), may hold values from 0 to 1023, as said below
Outputs:
- fine_out: float32 [9, 16, 512, 2048], P(None, None, 'gx', 'gy')
- coarse_out: float32 [9, 8, 256, 1024], P(None, None, 'gy', 'gx')
The draws below stay inside these ranges and needn't reach their ends.
Inputs may be any that keep to these rules, and one draw needn't show every extreme that they name: parent_rows[x] is x / 2 - 1 for x a positive multiple of 4, 0 for x = 0, x / 2 for x of remainder 2 by 4, (x - 1) / 2 or (x + 1) / 2 for remainder 1, and (x + 1) / 2 for remainder 3, never past the last coarse row. parent_cols[y] follows the same rule along columns, never past the last coarse column.
All inputs are finite; a program needn't handle non-finite values.
Results may differ from the reference program's by a relative error of at most 0.00002.
Values sent between devices are 32-bit elements; how exact they have to be, the bound alone decides.
A program may use at most 192 MiB of HBM per device.

```python
import math
import jax
import jax.numpy as jnp
from jax import lax

FZ = 16
CZ = 8
FINE_X = 512
FINE_Y = 2048
COARSE_X = 256
COARSE_Y = 1024


def parent_law(key, count, limit):
    flips = jax.random.randint(key, (count,), 0, 2).astype(jnp.int32)
    indices = jnp.arange(count).astype(jnp.int32)
    remain = indices % 4
    halves = indices // 2
    chosen = jnp.where(remain == 0, jnp.maximum(halves - 1, 0), jnp.where(remain == 2, halves, jnp.where(remain == 3, halves + 1, halves + flips)))
    return jnp.minimum(chosen, limit - 1).astype(jnp.int32)


def draw_parent_rows(key, part):
    return parent_law(jax.random.fold_in(key, 11), FINE_X, COARSE_X)


def draw_parent_cols(key, part):
    return parent_law(jax.random.fold_in(key, 23), FINE_Y, COARSE_Y)


def steps_of(rng, dims, pieces, least, largest):
    factor_of = 1.0
    for position, blocks in pieces:
        draws = jax.random.uniform(jax.random.fold_in(jax.random.fold_in(rng, 6), position), (blocks,), jnp.float32, least / len(pieces), largest / len(pieces))
        factor_of = factor_of * jnp.repeat(jnp.exp(draws), dims[position] // blocks).reshape((-1,) + (1,) * (len(dims) - 1 - position))
    return factor_of


def noise(key, dims, spread, bound, split=(), kind=jnp.bfloat16):
    loudness = steps_of(key, dims, split, -0.22, 0.18) if split else 1.0
    array = jax.random.normal(key, dims, jnp.float32) * spread * loudness
    return jnp.minimum(jnp.maximum(array, -bound), bound).astype(kind)


def setup_inputs(seed: int = 0) -> dict:
    streams_of = jax.random.split(jax.random.key(seed), 8)
    return {
        "fine_state": noise(streams_of[0], (9, FZ, FINE_X, FINE_Y), 1.0, 6.0, ((2, 8), (3, 16)), jnp.float32),
        "fine_medium": jnp.clip(jnp.exp(math.log(2.0) - 1.3862944 * jax.random.uniform(streams_of[1], (3, FZ, FINE_X, FINE_Y), jnp.float32) ** steps_of(streams_of[1], (3, FZ, FINE_X, FINE_Y), ((2, 8), (3, 16)), -0.2, 0.2)), 0.5, 2.0),
        "coarse_state": noise(streams_of[2], (9, CZ, COARSE_X, COARSE_Y), 1.0, 6.0, ((2, 16), (3, 8)), jnp.float32),
        "coarse_medium": jnp.clip(jnp.exp(math.log(2.0) - 1.3862944 * jax.random.uniform(streams_of[3], (3, CZ, COARSE_X, COARSE_Y), jnp.float32) ** steps_of(streams_of[3], (3, CZ, COARSE_X, COARSE_Y), ((2, 16), (3, 8)), -0.2, 0.2)), 0.5, 2.0),
        "coarse_past": noise(streams_of[4], (9, 2, COARSE_X, COARSE_Y), 1.0, 6.0, ((2, 16), (3, 8)), jnp.float32),
        "parent_rows": draw_parent_rows(jax.random.fold_in(streams_of[7], 71), 0),
        "parent_cols": draw_parent_cols(jax.random.fold_in(streams_of[7], 71), 0),
    }


COEFFS = (1225.0 / 1024.0, -245.0 / 3072.0, 49.0 / 5120.0, -5.0 / 7168.0)
STEP = 0.1


def derivative(values, dimension, forward, inv_spacing):
    rank_count = values.ndim
    dimension = dimension % rank_count
    cropped = values
    for other_dim in range(rank_count - 3, rank_count):
        if other_dim != dimension:
            cropped = lax.slice_in_dim(cropped, 4, cropped.shape[other_dim] - 4, axis=other_dim)
    length = cropped.shape[dimension] - 8
    result = None
    for tap_index in range(1, 5):
        upper_start = 4 + tap_index if forward else 3 + tap_index
        lower_start = 5 - tap_index if forward else 4 - tap_index
        upper_part = lax.slice_in_dim(cropped, upper_start, upper_start + length, axis=dimension)
        lower_part = lax.slice_in_dim(cropped, lower_start, lower_start + length, axis=dimension)
        tap_term = COEFFS[tap_index - 1] * (upper_part - lower_part)
        result = tap_term if result is None else result + tap_term
    return result * inv_spacing


def velocity_step(velocity, stress_pad, buoyancy, step_size, inv_spacing):
    first_rate = (derivative(stress_pad[0], -2, True, inv_spacing) + derivative(stress_pad[3], -1, False, inv_spacing)
                  + derivative(stress_pad[4], -3, False, inv_spacing))
    second_rate = (derivative(stress_pad[3], -2, False, inv_spacing) + derivative(stress_pad[1], -1, True, inv_spacing)
                   + derivative(stress_pad[5], -3, False, inv_spacing))
    third_rate = (derivative(stress_pad[4], -2, False, inv_spacing) + derivative(stress_pad[5], -1, False, inv_spacing)
                  + derivative(stress_pad[2], -3, True, inv_spacing))
    return velocity + step_size * buoyancy * jnp.stack([first_rate, second_rate, third_rate])


def stress_step(stress, velocity_pad, lame_first, shear_modulus, step_size, inv_spacing):
    strain_first = derivative(velocity_pad[0], -2, False, inv_spacing)
    strain_second = derivative(velocity_pad[1], -1, False, inv_spacing)
    strain_third = derivative(velocity_pad[2], -3, False, inv_spacing)
    dilation = strain_first + strain_second + strain_third
    rate_list = [
        lame_first * dilation + 2.0 * shear_modulus * strain_first,
        lame_first * dilation + 2.0 * shear_modulus * strain_second,
        lame_first * dilation + 2.0 * shear_modulus * strain_third,
        shear_modulus * (derivative(velocity_pad[0], -1, True, inv_spacing) + derivative(velocity_pad[1], -2, True, inv_spacing)),
        shear_modulus * (derivative(velocity_pad[0], -3, True, inv_spacing) + derivative(velocity_pad[2], -2, True, inv_spacing)),
        shear_modulus * (derivative(velocity_pad[1], -3, True, inv_spacing) + derivative(velocity_pad[2], -1, True, inv_spacing)),
    ]
    return stress + step_size * jnp.stack(rate_list)


def zero_layers(values, layer_count):
    return jnp.zeros((values.shape[0], layer_count) + values.shape[2:], values.dtype)


def fine_pad(values, ghost_cells):
    stacked = jnp.concatenate([zero_layers(values, 4), values, ghost_cells], axis=1)
    return jnp.pad(stacked, ((0, 0), (0, 0), (4, 4), (4, 4)))


def coarse_pad(values, ghost_cells):
    stacked = jnp.concatenate([ghost_cells, values, zero_layers(values, 4)], axis=1)
    return jnp.pad(stacked, ((0, 0), (0, 0), (4, 4), (4, 4)))


def reference(fine_state, fine_medium, coarse_state, coarse_medium, coarse_past, parent_rows, parent_cols):
    coarse_top = coarse_state[:, :2]
    time_levels = (coarse_top, 1.5 * coarse_top - 0.5 * coarse_past)
    fine_now = fine_state
    fine_depth = fine_state.shape[1]
    for coarse_level in time_levels:
        picked = jnp.take(jnp.take(coarse_level, parent_rows, axis=2), parent_cols, axis=3)
        ghost_cells = jnp.repeat(picked, 2, axis=1)
        velocity = velocity_step(fine_now[:3], fine_pad(fine_now[3:], ghost_cells[3:]), fine_medium[0], STEP, 1.0)
        stress = stress_step(fine_now[3:], fine_pad(velocity, ghost_cells[:3]), fine_medium[1], fine_medium[2], STEP, 1.0)
        fine_now = jnp.concatenate([velocity, stress], axis=0)
    blended = 0.5 * (fine_state[:, fine_depth - 8:] + fine_now[:, fine_depth - 8:])
    rows_half = blended.shape[2] // 2
    cols_half = blended.shape[3] // 2
    coarse_ghost = blended.reshape(9, 4, 2, rows_half, 2, cols_half, 2).mean(axis=(2, 4, 6))
    velocity = velocity_step(coarse_state[:3], coarse_pad(coarse_state[3:], coarse_ghost[3:]), coarse_medium[0], 2.0 * STEP, 0.5)
    stress = stress_step(coarse_state[3:], coarse_pad(velocity, coarse_ghost[:3]), coarse_medium[1], coarse_medium[2], 2.0 * STEP, 0.5)
    coarse_out = jnp.concatenate([velocity, stress], axis=0)
    return (fine_now, coarse_out)
```

```python
import jax
import jax.numpy as jnp
from jax import lax
from jax.experimental import pallas as pl
from jax.experimental.pallas import tpu as pltpu
from jax.sharding import PartitionSpec as P

C = (1225.0 / 1024.0, -245.0 / 3072.0, 49.0 / 5120.0, -5.0 / 7168.0)
SCALE = 0.1
MESH = pl.DeviceIdType.MESH
HI = lax.Precision.HIGHEST
F32 = jnp.float32

SX, SY, SYSIGN = (0, 3, 4), (3, 1, 5), (False, True, False)
VX, VY, VYSIGN = (0, 1, 2), (0, 1, 2), (True, False, True)


def lanes(shape):
    return lax.broadcasted_iota(jnp.int32, shape, len(shape) - 1)


def shifted(f, s):
    return f if s == 0 else pltpu.roll(f, (-s) % 128, f.ndim - 1)


def taps(get, fwd):
    out = None
    for k in range(1, 5):
        hi, lo = (k, 1 - k) if fwd else (k - 1, -k)
        term = C[k - 1] * (get(hi) - get(lo))
        out = term if out is None else out + term
    return out


def d_rows(buf, f, zz, r0, nr, fwd):
    return taps(lambda s: buf[f, zz, 8 + r0 + s : 8 + r0 + s + nr, :], fwd)


def d_layers(buf, f, zz, r0, nr, fwd):
    return taps(lambda s: buf[f, zz + s, 8 + r0 : 8 + r0 + nr, :], fwd)


def d_cols(buf, f, slot, corr, zz, zl, r0, nr, fwd):
    here = buf[f, zz, 8 + r0 : 8 + r0 + nr, :]
    inner = taps(lambda s: shifted(here, s), fwd)
    at = slot * 32 + zl * 4
    right = pltpu.roll(corr[0, r0 : r0 + nr, :], lax.rem(252 - at, 128), 1)
    left = pltpu.roll(corr[1, r0 : r0 + nr, :], lax.rem(256 - at, 128), 1)
    lane = lanes((nr, 128))
    edge = jnp.where(lane >= 124, right, jnp.where(lane < 4, left, 0.0))
    return inner + edge


def edge_weight(s, side, signs):
    lane = lanes((8, 128))
    j, field = lane & 3, lane >> 5
    inside = (j + s >= 0) & (j + s <= 3)

    def weight(fwd):
        if side == 0:
            k = (4 if fwd else 5) + s
            return C[k - 1] if 1 <= k <= 4 else 0.0
        k = (5 if fwd else 4) - s
        return -C[k - 1] if 1 <= k <= 4 else 0.0

    w = jnp.where(field == 0, weight(signs[0]), jnp.where(field == 1, weight(signs[1]), weight(signs[2])))
    return jnp.where(inside & (field < 3), w, 0.0)


def make_corr(corr, own, got, signs, nrow):
    for side in range(2):
        shifts = (0, -1, -2, -3) if side == 0 else (0, 1, 2, 3)
        weights = [edge_weight(s, side, signs) for s in shifts]

        def body(r, carry, side=side, shifts=shifts, weights=weights):
            rows = pl.ds(pl.multiple_of(r * 8, 8), 8)
            miss = got[1 - side, rows, :] - own[side, rows, :]
            total = None
            for s, w in zip(shifts, weights):
                term = w * shifted(miss, s)
                total = term if total is None else total + term
            corr[side, rows, :] = total
            return carry

        lax.fori_loop(0, nrow // 8, body, 0)


def pack_rows(buf, out, fields, z0, nrow):
    for i, f in enumerate(fields):
        for zl in range(8):
            half = 4 * (zl % 2)
            out[0, i, zl // 2, half : half + 4, :] = buf[f, 4 + z0 + zl, 8:12, :]
            out[1, i, zl // 2, half : half + 4, :] = buf[f, 4 + z0 + zl, 4 + nrow : 8 + nrow, :]


def unpack_rows(buf, got, fields, z0, nrow):
    for i, f in enumerate(fields):
        for zl in range(8):
            half = 4 * (zl % 2)
            buf[f, 4 + z0 + zl, 4:8, :] = got[0, i, zl // 2, half : half + 4, :]
            buf[f, 4 + z0 + zl, 8 + nrow : 12 + nrow, :] = got[1, i, zl // 2, half : half + 4, :]


def pack_cols(buf, out, fields, z0, nrow):
    lane = lanes((8, 128))

    def body(r, carry):
        src = pl.ds(pl.multiple_of(r * 8 + 8, 8), 8)
        first = jnp.zeros((8, 128), F32)
        last = jnp.zeros((8, 128), F32)
        for i, f in enumerate(fields):
            for zl in range(8):
                at = i * 32 + zl * 4
                here = buf[f, 4 + z0 + zl, src, :]
                mine = (lane >> 2) == (at >> 2)
                first = jnp.where(mine, shifted(here, -at), first)
                last = jnp.where(mine, shifted(here, 124 - at), last)
        dst = pl.ds(pl.multiple_of(r * 8, 8), 8)
        out[0, dst, :] = first
        out[1, dst, :] = last
        return carry

    lax.fori_loop(0, nrow // 8, body, 0)


def velocity_update(vb, sb, mb, corr, z0, n, nrow, zl0=0):
    nr = min(nrow, 16)

    def body(i, carry):
        zl = i + zl0
        z = z0 + zl
        zz = z + 4
        for r0 in range(0, nrow, nr):
            rows = slice(8 + r0, 8 + r0 + nr)
            b = mb[0, z, r0 : r0 + nr, :] * SCALE
            cols = lambda f, slot, fwd: d_cols(sb, f, slot, corr, zz, zl, r0, nr, fwd)
            row = lambda f, fwd: d_rows(sb, f, zz, r0, nr, fwd)
            lay = lambda f, fwd: d_layers(sb, f, zz, r0, nr, fwd)
            vb[0, zz, rows, :] = vb[0, zz, rows, :] + b * (row(0, True) + cols(3, 0, False) + lay(4, False))
            vb[1, zz, rows, :] = vb[1, zz, rows, :] + b * (row(3, False) + cols(1, 1, True) + lay(5, False))
            vb[2, zz, rows, :] = vb[2, zz, rows, :] + b * (row(4, False) + cols(5, 2, False) + lay(2, True))
        return carry

    lax.fori_loop(0, n, body, 0)


def stress_update(vb, sb, mb, corr, z0, n, nrow, zl0=0):
    nr = min(nrow, 16)

    def body(i, carry):
        zl = i + zl0
        z = z0 + zl
        zz = z + 4
        for r0 in range(0, nrow, nr):
            rows = slice(8 + r0, 8 + r0 + nr)
            lam = mb[1, z, r0 : r0 + nr, :] * SCALE
            mu = mb[2, z, r0 : r0 + nr, :] * SCALE
            cols = lambda f, fwd: d_cols(vb, f, f, corr, zz, zl, r0, nr, fwd)
            row = lambda f, fwd: d_rows(vb, f, zz, r0, nr, fwd)
            lay = lambda f, fwd: d_layers(vb, f, zz, r0, nr, fwd)
            exx, eyy, ezz = row(0, False), cols(1, False), lay(2, False)
            dil = lam * (exx + eyy + ezz)
            two = mu + mu
            sb[0, zz, rows, :] = sb[0, zz, rows, :] + (dil + two * exx)
            sb[1, zz, rows, :] = sb[1, zz, rows, :] + (dil + two * eyy)
            sb[2, zz, rows, :] = sb[2, zz, rows, :] + (dil + two * ezz)
            sb[3, zz, rows, :] = sb[3, zz, rows, :] + mu * (cols(0, True) + row(1, True))
            sb[4, zz, rows, :] = sb[4, zz, rows, :] + mu * (lay(0, True) + row(2, True))
            sb[5, zz, rows, :] = sb[5, zz, rows, :] + mu * (lay(1, True) + cols(2, True))
        return carry

    lax.fori_loop(0, n, body, 0)


N_MSG = 64
ID_FINE, ID_CS, ID_CV, ID_MAIN, ID_FAR, ID_ROW, ID_KNOT, ID_LIFT = 0, 32, 36, 40, 42, 44, 46, 48


def kernel(
    nx, ny, fs, fm, cs, cm, cp, prow, pcol, fout, cout,
    vb, sb, mb, old, xs, xr, ys, yr, corr,
    cvb, csb, cmb, cpb, cxs, cxr, cys, cyr, ccorr,
    send_main, send_far, send_row, send_knot, got_main, got_far, got_row, got_knot,
    stack, wide, planes, half, pairs, send_lift, got_lift,
    send_sem, recv_sem, load_sem, out_sem,
):
    gx = lax.axis_index("gx")
    gy = lax.axis_index("gy")
    up, down = gx > 0, gx < nx - 1
    left, right = gy > 0, gy < ny - 1
    oc, par = gy // 2, lax.rem(gy, 2)
    even = par == 0
    far_c = jnp.where(even, oc - 1, oc + 1)
    has_far = jnp.logical_and(far_c >= 0, far_c <= nx - 1)
    slot_out = 1 - par
    row_t = oc + 2 * par - 1
    has_row_t = jnp.logical_and(row_t >= 0, row_t <= nx - 1)

    def is_me(t):
        return jnp.logical_and(t[0] == gx, t[1] == gy)

    true = gx >= 0
    sent = []

    def send(src, dst, sid, rid, target, cond, maybe_self=False):
        remote = jnp.logical_and(cond, jnp.logical_not(is_me(target))) if maybe_self else cond

        def copy():
            return pltpu.make_async_remote_copy(
                src_ref=src, dst_ref=dst, send_sem=send_sem.at[sid], recv_sem=recv_sem.at[rid],
                device_id=target, device_id_type=MESH,
            )

        @pl.when(remote)
        def _():
            copy().start()

        if maybe_self:

            @pl.when(jnp.logical_and(cond, is_me(target)))
            def _():
                pltpu.make_async_copy(src, dst, recv_sem.at[rid]).start()

        sent.append((remote, copy))

    def receive(dst, rid, cond=None):
        def wait():
            pltpu.make_async_copy(dst, dst, recv_sem.at[rid]).wait()

        if cond is None:
            wait()
        else:
            pl.when(cond)(wait)

    loads = [
        pltpu.make_async_copy(cs.at[0:3], cvb.at[:, 4:12, 8:24, :], load_sem.at[0]),
        pltpu.make_async_copy(cs.at[3:9], csb.at[:, 4:12, 8:24, :], load_sem.at[1]),
        pltpu.make_async_copy(cp, cpb, load_sem.at[2]),
        pltpu.make_async_copy(fs.at[3:9], sb.at[:, 4:20, 8:72, :], load_sem.at[3]),
        pltpu.make_async_copy(fs.at[0:3], vb.at[:, 4:20, 8:72, :], load_sem.at[4]),
        pltpu.make_async_copy(fm, mb, load_sem.at[5]),
        pltpu.make_async_copy(fs.at[0:3, 8:16], old.at[0:3], load_sem.at[6]),
        pltpu.make_async_copy(fs.at[5, 8:16], old.at[3], load_sem.at[7]),
        pltpu.make_async_copy(fs.at[7:9, 8:16], old.at[4:6], load_sem.at[8]),
        pltpu.make_async_copy(cm, cmb, load_sem.at[9]),
    ]
    for load in loads:
        load.start()

    barrier = pltpu.get_barrier_semaphore()

    def greet(target, cond, maybe_self=False):
        if maybe_self:
            cond = jnp.logical_and(cond, jnp.logical_not(is_me(target)))

        @pl.when(cond)
        def _():
            pl.semaphore_signal(barrier, inc=1, device_id=target, device_id_type=MESH)

    def count(target, cond, maybe_self=False):
        if maybe_self:
            cond = jnp.logical_and(cond, jnp.logical_not(is_me(target)))
        return jnp.where(cond, 1, 0)

    near = [((gx - 1, gy), up), ((gx + 1, gy), down), ((gx, gy - 1), left), ((gx, gy + 1), right)]
    owners = [(oc, 2 * gx), (oc, 2 * gx + 1)]
    for target, cond in near:
        greet(target, cond)
    for target in owners:
        greet(target, true, True)
        greet((far_c, target[1]), has_far)
    top_ok, bot_ok = up, down
    greet((oc, 2 * gx - 1), top_ok)
    greet((oc, 2 * gx + 2), bot_ok)
    greet((far_c, 2 * gx - 1), jnp.logical_and(top_ok, has_far), True)
    greet((far_c, 2 * gx + 2), jnp.logical_and(bot_ok, has_far), True)

    a = oc
    main_t = owners
    far_t = [((a, 2 * gx - 1), gx > 0), ((a, 2 * gx + 2), gx < nx - 1)]
    row_ts = [((row_t, 2 * gx), has_row_t), ((row_t, 2 * gx + 1), has_row_t)]
    knot_t = [
        ((row_t, 2 * gx - 1), jnp.logical_and(has_row_t, gx > 0)),
        ((row_t, 2 * gx + 2), jnp.logical_and(has_row_t, gx < nx - 1)),
    ]
    expected = jnp.int32(0)
    for target, cond in near:
        expected = expected + count(target, cond)
    for target in owners:
        expected = expected + count(target, true, True)
    for target, cond in far_t:
        expected = expected + count(target, cond)
    for target, cond in row_ts:
        expected = expected + count(target, cond)
    for target, cond in knot_t:
        expected = expected + count(target, cond, True)

    def clear(ref):
        ref[...] = jnp.zeros(ref.shape, F32)

    for cond, row_slot in ((up, 0), (down, 1)):

        @pl.when(jnp.logical_not(cond))
        def _(row_slot=row_slot):
            for e in range(8):
                clear(xr.at[e, row_slot])
            for e in range(2):
                clear(cyr.at[e, row_slot])

    for cond, col_slot in ((left, 0), (right, 1)):

        @pl.when(jnp.logical_not(cond))
        def _(col_slot=col_slot):
            for e in range(8):
                clear(yr.at[e, col_slot])
            for e in range(2):
                clear(cxr.at[e, col_slot])

    for f in range(3):
        vb[f, 0:4, 8:72, :] = jnp.zeros((4, 64, 128), F32)
        cvb[f, 12:16, 8:24, :] = jnp.zeros((4, 16, 128), F32)
    for f in (2, 4, 5):
        sb[f, 0:4, 8:72, :] = jnp.zeros((4, 64, 128), F32)
        csb[f, 12:16, 8:24, :] = jnp.zeros((4, 16, 128), F32)

    @pl.when(jnp.logical_not(has_far))
    def _():
        clear(got_far)

    for slot, cond in ((0, up), (1, down)):

        @pl.when(jnp.logical_not(jnp.logical_and(cond, has_far)))
        def _(slot=slot):
            clear(got_knot.at[slot])

    loads[0].wait()
    loads[1].wait()
    loads[2].wait()
    lane16 = lanes((16, 128))
    low = lane16 < 64
    tile_near = [jnp.zeros((16, 128), F32), jnp.zeros((16, 128), F32)]
    tile_far = [jnp.zeros((16, 128), F32), jnp.zeros((16, 128), F32)]
    for s in range(2):
        for f6 in range(6):
            p = s * 6 + f6
            buf, f, fp = (cvb, f6, f6) if f6 < 3 else (csb, (2, 4, 5)[f6 - 3], (5, 7, 8)[f6 - 3])
            layer = []
            for m in range(2):
                plane = buf[f, 4 + m, 8:24, :]
                if s == 1:
                    plane = 1.5 * plane - 0.5 * cpb[fp, m, :, :]
                layer.append(plane)
                q = 2 * p + m
                here = lane16 == q
                tile_near[0] = jnp.where(here, shifted(plane, 64 - q), tile_near[0])
                tile_near[1] = jnp.where(here, shifted(plane, 63 - q), tile_near[1])
                tile_far[0] = jnp.where(here, shifted(plane, -q), tile_far[0])
                tile_far[1] = jnp.where(here, shifted(plane, 127 - q), tile_far[1])
            send_main[0, p, :, :] = jnp.where(low, layer[0], shifted(layer[1], 64))
            send_main[1, p, :, :] = jnp.where(low, shifted(layer[0], 64), layer[1])
    for side in range(2):
        send_main[side, 12, :, :] = tile_near[side]
        send_far[side, :, :] = tile_far[side]

    for dd, row in ((0, 0), (1, 15)):

        @pl.when(par == dd)
        def _(row=row):
            for side in range(2):
                for p in range(13):
                    send_row[side, p : p + 1, :] = send_main[side, p, row : row + 1, :]
                send_knot[side, 0:1, :] = send_far[side, row : row + 1, :]

    pl.semaphore_wait(barrier, expected)

    for side in range(2):
        send(send_main.at[side], got_main.at[par], ID_MAIN + side, ID_MAIN + par, main_t[side], true, True)
        send(send_far.at[side], got_far.at[par], ID_FAR + side, ID_FAR + par, *far_t[side])
        send(send_row.at[side], got_row.at[slot_out], ID_ROW + side, ID_ROW + slot_out, *row_ts[side])
        send(send_knot.at[side], got_knot.at[slot_out], ID_KNOT + side, ID_KNOT + slot_out, *knot_t[side], True)

    def fine_send(e, ch, buf, xf, yf):
        m = 2 * e + ch
        pack_rows(buf, xs.at[m], xf, 8 * ch, 64)
        pack_cols(buf, ys.at[m], yf, 8 * ch, 64)
        i = ID_FINE + 4 * m
        send(xs.at[m, 0], xr.at[m, 1], i, i + 1, *near[0])
        send(xs.at[m, 1], xr.at[m, 0], i + 1, i, *near[1])
        send(ys.at[m, 0], yr.at[m, 1], i + 2, i + 3, *near[2])
        send(ys.at[m, 1], yr.at[m, 0], i + 3, i + 2, *near[3])

    def fine_receive(e, ch, buf, xf, signs):
        m = 2 * e + ch
        i = ID_FINE + 4 * m
        receive(xr.at[m, 0], i, up)
        receive(xr.at[m, 1], i + 1, down)
        unpack_rows(buf, xr.at[m], xf, 8 * ch, 64)
        receive(yr.at[m, 0], i + 2, left)
        receive(yr.at[m, 1], i + 3, right)
        make_corr(corr, ys.at[m], yr.at[m], signs, 64)

    def coarse_send(e, buf, xf, yf):
        pack_rows(buf, cxs.at[e], xf, 0, 16)
        pack_cols(buf, cys.at[e], yf, 0, 16)
        i = ID_CS + 4 * e
        send(cxs.at[e, 0], cxr.at[e, 1], i, i + 1, *near[2])
        send(cxs.at[e, 1], cxr.at[e, 0], i + 1, i, *near[3])
        send(cys.at[e, 0], cyr.at[e, 1], i + 2, i + 3, *near[0])
        send(cys.at[e, 1], cyr.at[e, 0], i + 3, i + 2, *near[1])

    def coarse_receive(e, buf, xf, signs):
        i = ID_CS + 4 * e
        receive(cxr.at[e, 0], i, left)
        receive(cxr.at[e, 1], i + 1, right)
        unpack_rows(buf, cxr.at[e], xf, 0, 16)
        receive(cyr.at[e, 0], i + 2, up)
        receive(cyr.at[e, 1], i + 3, down)
        make_corr(ccorr, cys.at[e], cyr.at[e], signs, 16)

    loads[3].wait()
    fine_send(0, 0, sb, SX, SY)
    fine_send(0, 1, sb, SX, SY)
    coarse_send(0, csb, SX, SY)
    loads[4].wait()
    loads[5].wait()

    fine_receive(0, 0, sb, SX, SYSIGN)
    velocity_update(vb, sb, mb, corr, 0, 8, 64)
    fine_send(1, 0, vb, VX, VY)

    receive(got_main.at[0], ID_MAIN)
    receive(got_main.at[1], ID_MAIN + 1)
    receive(got_far.at[0], ID_FAR, has_far)
    receive(got_far.at[1], ID_FAR + 1, has_far)
    receive(got_row.at[0], ID_ROW, top_ok)
    receive(got_row.at[1], ID_ROW + 1, bot_ok)
    receive(got_knot.at[0], ID_KNOT, jnp.logical_and(top_ok, has_far))
    receive(got_knot.at[1], ID_KNOT + 1, jnp.logical_and(bot_ok, has_far))
    for h in range(2):
        for p in range(13):
            stack[p, 1 + 16 * h : 17 + 16 * h, :] = got_main[h, p, :, :]
        stack[13, 1 + 16 * h : 17 + 16 * h, :] = got_far[h, :, :]

    for h, row, src_row, ok in ((0, 0, 0, top_ok), (1, 33, 15, bot_ok)):

        @pl.when(ok)
        def _(h=h, row=row):
            for p in range(13):
                stack[p, row : row + 1, :] = got_row[h, p : p + 1, :]
            stack[13, row : row + 1, :] = got_knot[h, 0:1, :]

        @pl.when(jnp.logical_not(ok))
        def _(h=h, row=row, src_row=src_row):
            for p in range(13):
                stack[p, row : row + 1, :] = got_main[h, p, src_row : src_row + 1, :]
            stack[13, row : row + 1, :] = got_far[h, src_row : src_row + 1, :]

    row16 = lax.broadcasted_iota(jnp.int32, (16, 128), 0)
    flips = jnp.zeros((16, 128), jnp.int32)
    for k in range(16):
        flips = jnp.where(row16 == k, prow[4 * k + 1] - gx * 32 - 2 * k, flips)
    flipped = flips == 1
    for p in range(14):
        wide[p, pl.ds(0, 16, stride=4), :] = stack[p, pl.ds(0, 16, stride=2), :]
        wide[p, pl.ds(1, 16, stride=4), :] = jnp.where(
            flipped, stack[p, pl.ds(2, 16, stride=2), :], stack[p, pl.ds(1, 16, stride=2), :]
        )
        wide[p, pl.ds(2, 16, stride=4), :] = stack[p, pl.ds(2, 16, stride=2), :]
        wide[p, pl.ds(3, 16, stride=4), :] = stack[p, pl.ds(3, 16, stride=2), :]

    col = jnp.clip(pcol[...].reshape(1, 128) - gy * 64, 0, 63)
    src_lane = lax.broadcasted_iota(jnp.int32, (128, 128), 0)
    pick0 = jnp.where(src_lane == col, 1.0, 0.0).astype(F32)
    pick1 = jnp.where(src_lane == col + 64, 1.0, 0.0).astype(F32)
    pick = jnp.concatenate([pick0, pick1], axis=1)
    lane64 = lanes((64, 128))
    at_first = jnp.logical_and(lane64 == 0, left)
    at_last = jnp.logical_and(lane64 == 127, right)

    first_ring = jnp.where(even, wide[13, :, :], wide[12, :, :])
    last_ring = jnp.where(even, wide[12, :, :], wide[13, :, :])
    half[0, :, :] = first_ring
    half[1, :, :] = last_ring

    def expand(p, carry):
        both = jnp.dot(wide[p, :, :], pick, precision=HI, preferred_element_type=F32)
        for m in range(2):
            plane = both[:, 128 * m : 128 * m + 128]
            q = 2 * p + m
            one = pltpu.roll(half[0, :, :], lax.rem(128 - q, 128), 1)
            two = pltpu.roll(half[1, :, :], 127 - q, 1)
            planes[q, :, :] = jnp.where(at_first, one, jnp.where(at_last, two, plane))
        return carry

    lax.fori_loop(0, 12, expand, 0)

    def place(s):
        for f6 in range(6):
            buf, f = (vb, f6) if f6 < 3 else (sb, (2, 4, 5)[f6 - 3])
            for g in range(4):
                buf[f, 20 + g, 8:72, :] = planes[2 * (s * 6 + f6) + g // 2, :, :]

    place(0)

    fine_receive(0, 1, sb, SX, SYSIGN)
    velocity_update(vb, sb, mb, corr, 8, 8, 64)
    fine_send(1, 1, vb, VX, VY)
    coarse_receive(0, csb, SX, SYSIGN)

    fine_receive(1, 0, vb, VX, VYSIGN)
    stress_update(vb, sb, mb, corr, 0, 8, 64)
    fine_send(2, 0, sb, SX, SY)
    fine_receive(1, 1, vb, VX, VYSIGN)
    stress_update(vb, sb, mb, corr, 8, 8, 64)
    fine_send(2, 1, sb, SX, SY)
    place(1)

    outs = []

    def emit(src, dst):
        copy = pltpu.make_async_copy(src, dst, out_sem.at[len(outs)])
        copy.start()
        outs.append(copy)

    fine_receive(2, 0, sb, SX, SYSIGN)
    velocity_update(vb, sb, mb, corr, 0, 8, 64)
    fine_send(3, 0, vb, VX, VY)
    fine_receive(2, 1, sb, SX, SYSIGN)
    velocity_update(vb, sb, mb, corr, 8, 8, 64)
    fine_send(3, 1, vb, VX, VY)
    emit(vb.at[:, 4:20, 8:72, :], fout.at[0:3])

    tgt_lane = lanes((128, 128))
    even_pick = jnp.where(tgt_lane == src_lane // 2, 0.0625, 0.0).astype(F32)
    odd_pick = jnp.where(tgt_lane == 64 + src_lane // 2, 0.0625, 0.0).astype(F32)

    def lift(kind, buf, fields):
        for i, f in enumerate(fields):
            for m in range(4):
                half[0, :, :] = (
                    old[3 * kind + i, 2 * m, :, :] + old[3 * kind + i, 2 * m + 1, :, :]
                    + buf[f, 12 + 2 * m, 8:72, :] + buf[f, 13 + 2 * m, 8:72, :]
                )
                summed = half[0, pl.ds(0, 32, stride=2), :] + half[0, pl.ds(1, 32, stride=2), :]
                at = 32 * (2 * i + m // 2)
                pairs[m % 2, at : at + 32, :] = summed
        packed = jnp.dot(pairs[0, :, :], even_pick, precision=HI, preferred_element_type=F32) + jnp.dot(
            pairs[1, :, :], odd_pick, precision=HI, preferred_element_type=F32
        )
        for i in range(6):
            for dd in range(2):
                send_lift[kind, dd, i, :, :] = packed[32 * i + 16 * dd : 32 * i + 16 * dd + 16, :]
        for dd in range(2):
            sid = ID_LIFT + 2 * kind
            send(send_lift.at[kind, dd], got_lift.at[kind, par], sid + dd, sid + par, owners[dd], true, True)

    def settle(kind, buf, fields):
        for h in range(2):
            receive(got_lift.at[kind, h], ID_LIFT + 2 * kind + h)
        for i, f in enumerate(fields):
            for mm in range(2):
                e_pack = got_lift[kind, 0, 2 * i + mm, :, :]
                o_pack = got_lift[kind, 1, 2 * i + mm, :, :]
                buf[f, 2 * mm, 8:24, :] = jnp.where(low, e_pack, shifted(o_pack, 64))
                buf[f, 2 * mm + 1, 8:24, :] = jnp.where(low, shifted(e_pack, 64), o_pack)

    for i in (6, 7, 8):
        loads[i].wait()
    lift(0, vb, (0, 1, 2))

    fine_receive(3, 1, vb, VX, VYSIGN)
    stress_update(vb, sb, mb, corr, 8, 8, 64)
    lift(1, sb, (2, 4, 5))
    emit(sb.at[:, 12:20, 8:72, :], fout.at[3:9, 8:16])
    fine_receive(3, 0, vb, VX, VYSIGN)
    stress_update(vb, sb, mb, corr, 0, 8, 64)
    emit(sb.at[:, 4:12, 8:72, :], fout.at[3:9, 0:8])

    loads[9].wait()
    settle(0, cvb, (0, 1, 2))
    settle(1, csb, (2, 4, 5))
    velocity_update(cvb, csb, cmb, ccorr, 0, 8, 16)
    coarse_send(1, cvb, VX, VY)
    emit(cvb.at[:, 4:12, 8:24, :], cout.at[0:3])
    coarse_receive(1, cvb, VX, VYSIGN)
    stress_update(cvb, csb, cmb, ccorr, 0, 8, 16)
    emit(csb.at[:, 4:12, 8:24, :], cout.at[3:9])

    for copy in outs:
        copy.wait()
    for cond, copy in sent:

        @pl.when(cond)
        def _(copy=copy):
            copy().wait_send()


def solution(mesh):
    nx, ny = mesh.shape["gx"], mesh.shape["gy"]

    def body(fs, fm, cs, cm, cp, prow, pcol):
        any_spec = pl.BlockSpec(memory_space=pl.ANY)

        def v(*shape):
            return pltpu.VMEM(shape, F32)

        def call(*refs):
            kernel(nx, ny, *refs)

        return pl.pallas_call(
            call,
            out_shape=(jax.ShapeDtypeStruct(fs.shape, F32), jax.ShapeDtypeStruct(cs.shape, F32)),
            in_specs=[any_spec] * 5
            + [pl.BlockSpec(memory_space=pltpu.SMEM), pl.BlockSpec(memory_space=pltpu.VMEM)],
            out_specs=(any_spec, any_spec),
            scratch_shapes=[
                v(3, 24, 80, 128), v(6, 24, 80, 128), v(3, 16, 64, 128), v(6, 8, 64, 128),
                v(8, 2, 3, 4, 8, 128), v(8, 2, 3, 4, 8, 128), v(8, 2, 64, 128), v(8, 2, 64, 128), v(2, 64, 128),
                v(3, 16, 32, 128), v(6, 16, 32, 128), v(3, 8, 16, 128), v(9, 2, 16, 128),
                v(2, 2, 3, 4, 8, 128), v(2, 2, 3, 4, 8, 128), v(2, 2, 16, 128), v(2, 2, 16, 128), v(2, 16, 128),
                v(2, 13, 16, 128), v(2, 16, 128), v(2, 16, 128), v(2, 8, 128),
                v(2, 13, 16, 128), v(2, 16, 128), v(2, 16, 128), v(2, 8, 128),
                v(14, 40, 128), v(14, 64, 128), v(24, 64, 128), v(2, 64, 128), v(2, 192, 128),
                v(2, 2, 6, 16, 128), v(2, 2, 6, 16, 128),
                pltpu.SemaphoreType.DMA((N_MSG,)), pltpu.SemaphoreType.DMA((N_MSG,)),
                pltpu.SemaphoreType.DMA((10,)), pltpu.SemaphoreType.DMA((8,)),
            ],
            compiler_params=pltpu.CompilerParams(collective_id=0, has_side_effects=True),
            name="slabs",
        )(fs, fm, cs, cm, cp, prow, pcol)

    return jax.shard_map(
        body,
        mesh=mesh,
        in_specs=(
            P(None, None, "gx", "gy"),
            P(None, None, "gx", "gy"),
            P(None, None, "gy", "gx"),
            P(None, None, "gy", "gx"),
            P(None, None, "gy", "gx"),
            P("gx"),
            P("gy"),
        ),
        out_specs=(P(None, None, "gx", "gy"), P(None, None, "gy", "gx")),
        check_vma=False,
    )
```
